256 devices in a mesh: dp: 32 (over z, x_hi, core), mp: 8 (over y, x_lo).
Axes of the slice: x: 4 (x_hi: 2, x_lo: 2; x = x_hi * 2 + x_lo), y: 4, z: 8, core: 2. Of those that a mesh axis runs over, the one named last changes fastest.
Arguments:
- activations: bfloat16 [2, 4096, 3968], P(None, 'dp'), may hold values from -6 to 6
- out_grads: bfloat16 [2, 4096, 3968], P(None, 'dp', 'mp'), may hold values from -0.29882812 to 0.29882812
- error_memory: bfloat16 [126976, 3968], P('dp', 'mp'), may hold values from -6 to 6
- q_previous: float32 [3968, 32], P('mp'), may hold values from -6 to 6
Outputs:
- new_error: bfloat16 [126976, 3968], P('dp', 'mp')
- p_basis: float32 [3968, 32], P('dp')
- q_factor: float32 [3968, 32], P('mp')
The draws below stay inside these ranges and needn't reach their ends.
All inputs are finite; a program needn't handle non-finite values.
Results may differ from the reference program's by a relative error of at most 0.001.
Values sent between devices are 32-bit elements; how exact they have to be, the bound alone decides.
A program may use at most 64 MiB of HBM per device.

```python
import jax
import jax.numpy as jnp
from jax import lax

D = 3968
R = 32
MICRO = 2
TOK_DEV = 128
TOKENS = 4096
F = 3968
ERR_ROWS = 126976
N_DP = 32


def levels(stream_key, shape, split, smallest, top_value):
    level = 1.0
    for position, blocks in split:
        heights = jax.random.uniform(jax.random.fold_in(jax.random.fold_in(stream_key, 6), position), (blocks,), jnp.float32, smallest / len(split), top_value / len(split))
        level = level * jnp.repeat(jnp.exp(heights), shape[position] // blocks).reshape((-1,) + (1,) * (len(shape) - 1 - position))
    return level


def scatter_about(own_key, shape, deviation, limit, cuts=(), dtype=jnp.bfloat16):
    drawn = jax.random.normal(own_key, shape, jnp.float32) * deviation
    if len(cuts) > 0:
        drawn = levels(own_key, shape, cuts, -0.22, 0.18) * drawn
    return jnp.clip(drawn, min=-limit, max=limit).astype(dtype)


def setup_inputs(seed: int = 0) -> dict:
    splits = jax.random.split(jax.random.key(seed), 5)
    return {
        "activations": scatter_about(splits[0], (MICRO, TOKENS, D), 1.0, 6.0, ((1, 32),)),
        "out_grads": scatter_about(splits[1], (MICRO, TOKENS, F), 0.044, 0.29882812, ((1, 32), (2, 8))),
        "error_memory": scatter_about(splits[2], (ERR_ROWS, F), 1.0, 6.0, ((0, 32), (1, 8))),
        "q_previous": scatter_about(splits[3], (F, R), 1.0, 6.0, ((0, 8),), jnp.float32),
    }


def reference(activations, out_grads, error_memory, q_previous):
    acts_all = activations.reshape(MICRO, N_DP, TOK_DEV, D).transpose(1, 0, 2, 3).reshape(N_DP, MICRO * TOK_DEV, D)
    grads_all = out_grads.reshape(MICRO, N_DP, TOK_DEV, F).transpose(1, 0, 2, 3).reshape(N_DP, MICRO * TOK_DEV, F)
    errors_all = error_memory.reshape(N_DP, D, F)

    def form_merged(items):
        token_rows, grad_rows, memory = items
        product = jnp.einsum('td,tf->df', token_rows.astype(jnp.float32), grad_rows.astype(jnp.float32), preferred_element_type=jnp.float32)
        return product + memory.astype(jnp.float32)
    merged_all = lax.map(form_merged, (acts_all, grads_all, errors_all))
    p_whole = jnp.einsum('idf,fr->dr', merged_all, q_previous, precision=lax.Precision.HIGHEST)
    gram_total = jnp.dot(p_whole.T, p_whole, precision=lax.Precision.HIGHEST)
    lower_factor = jnp.linalg.cholesky(gram_total)
    p_basis = jax.scipy.linalg.solve_triangular(lower_factor, p_whole.T, lower=True).T
    q_factor = jnp.einsum('idf,dr->fr', merged_all, p_basis, precision=lax.Precision.HIGHEST) / N_DP
    approx = jnp.dot(p_basis, q_factor.T, precision=lax.Precision.HIGHEST)
    new_error = (merged_all - approx[None]).astype(jnp.bfloat16).reshape(N_DP * D, F)
    return (new_error, p_basis, q_factor)
```

```python
import functools

import jax
import jax.numpy as jnp
from jax import lax
from jax.experimental import pallas as pl
from jax.experimental.pallas import tpu as pltpu
from jax.sharding import PartitionSpec as P

MESH = pl.DeviceIdType.MESH
F32 = jnp.float32
BF16 = jnp.bfloat16
BLOCKS = 16
LANES = 256


def split3(x):
    high = x.astype(BF16)
    rest = x - high.astype(F32)
    middle = rest.astype(BF16)
    low = (rest - middle.astype(F32)).astype(BF16)
    return jnp.concatenate([high, middle, low], axis=0)


def fold3(x):
    rows = x.shape[0] // 3
    return x[:rows] + x[rows : 2 * rows] + x[2 * rows :]


def dot_nn(a, b):
    return lax.dot_general(a, b, (((1,), (0,)), ((), ())), preferred_element_type=F32)


def dot_nt(a, b, precision=None):
    return lax.dot_general(
        a, b, (((1,), (1,)), ((), ())), preferred_element_type=F32, precision=precision
    )


def inverse_factor(gram):
    n = gram.shape[0]
    rows = lax.broadcasted_iota(jnp.int32, (n, 2 * n), 0)
    columns = lax.broadcasted_iota(jnp.int32, (n, 2 * n), 1)
    identity = jnp.where(rows + n == columns, 1.0, 0.0).astype(F32)
    wide = jnp.where(columns < n, jnp.concatenate([gram, gram], axis=1), identity)
    row_index = lax.broadcasted_iota(jnp.int32, (n, 1), 0)
    for j in range(n):
        pivot = wide[j : j + 1, j : j + 1]
        scale = lax.rsqrt(pivot)
        scale = scale * (1.5 - 0.5 * pivot * scale * scale)
        row = wide[j : j + 1, :] * scale
        factor = wide[:, j : j + 1] * scale
        below = wide - factor * row
        wide = jnp.where(row_index > j, below, jnp.where(row_index == j, row, wide))
    return wide[:, n:]


def reduce_kernel(
    q_hbm, g_hbm, a_hbm, e_hbm,
    merged_ref, basis3_ref, q3_ref, qt_ref, pb_ref,
    qv, gv, av, ev,
    p_part, c_recv, x_src, x_recv, z_buf, p_full, ps,
    w_src, w_recv, w_z, w_full, basis_f,
    load_sem, ssem, rsem,
):
    rank = qv.shape[0]
    half = rank // 2
    width = e_hbm.shape[1]
    share = pb_ref.shape[1]
    dp, mp = lax.axis_index("dp"), lax.axis_index("mp")
    mz, mxh, mc = dp // 4, (dp // 2) % 2, dp % 2
    my, mxl = mp // 2, mp % 2
    mx = mxh * 2 + mxl
    me = my * 4 + mx

    def device(x, y, z, c):
        return ((z * 2 + x // 2) * 2 + c, y * 2 + x % 2)

    def plane_peer(j):
        return (mx + j % 4) % 4, (my + j // 4) % 4

    def group_peer(j):
        return (mxh + j // 2) % 2, (mc + j % 2) % 2

    partner = device(mx, my, mz, (mc + 1) % 2)

    tokens = a_hbm.shape[1]
    loads = [pltpu.make_async_copy(q_hbm, qv, load_sem.at[0])]
    loads[0].start()
    g_loads = []
    for m in range(2):
        cp = pltpu.make_async_copy(g_hbm.at[m], gv.at[:, pl.ds(m * tokens, tokens)], load_sem.at[1 + m])
        cp.start()
        g_loads.append(cp)
    step = 1024
    pieces = [(s, min(step, width - s)) for s in range(0, width, step)]
    piece_loads = []
    for i, (s, n) in enumerate(pieces):
        own = []
        for m in range(2):
            own.append(
                pltpu.make_async_copy(
                    a_hbm.at[m, :, pl.ds(s, n)], av.at[pl.ds(m * tokens, tokens), pl.ds(s, n)], load_sem.at[3 + 3 * i + m]
                )
            )
        own.append(
            pltpu.make_async_copy(e_hbm.at[:, pl.ds(s, n)], ev.at[:, pl.ds(s, n)], load_sem.at[5 + 3 * i])
        )
        for cp in own:
            cp.start()
        piece_loads.append(own)

    barrier = pltpu.get_barrier_semaphore()

    def greet(target):
        pl.semaphore_signal(barrier, inc=1, device_id=target, device_id_type=MESH)

    greet(partner)

    def greet_plane(j, carry):
        x, y = plane_peer(j)
        greet(device(x, y, mz, mc))
        return carry

    lax.fori_loop(1, 16, greet_plane, 0)

    def greet_z(j, carry):
        greet(device(mx, my, (mz + j) % 8, mc))
        return carry

    lax.fori_loop(1, 8, greet_z, 0)
    greet(device(((mxh + 1) % 2) * 2 + mxl, my, mz, (mc + 1) % 2))

    padded = ev.shape[1]
    ev[:, width:] = jnp.zeros((ev.shape[0], padded - width), BF16)
    av[:, width:] = jnp.zeros((av.shape[0], padded - width), BF16)

    loads[0].wait()
    qs = split3(qv[...])
    for cp in g_loads:
        cp.wait()
    gqs = split3(fold3(dot_nn(qs, gv[...])))
    for i, (s, n) in enumerate(pieces):
        for cp in piece_loads[i]:
            cp.wait()
        n = min(step, padded - s)
        r = fold3(dot_nn(qs, ev[:, s : s + n]) + dot_nn(gqs, av[:, s : s + n]))
        for b in range(n // LANES):
            p_part[s // LANES + b] = r[:, b * LANES : (b + 1) * LANES]

    pl.semaphore_wait(barrier, 24)

    def remote(src, dst, phase, target):
        return pltpu.make_async_remote_copy(
            src_ref=src, dst_ref=dst, send_sem=ssem.at[phase], recv_sem=rsem.at[phase],
            device_id=target, device_id_type=MESH,
        )

    mine = pl.ds(pl.multiple_of(mc * half, half), half)
    other = pl.ds(pl.multiple_of(((mc + 1) % 2) * half, half), half)

    swap = remote(p_part.at[:, other, :], c_recv, 0, partner)
    swap.start()
    swap.wait_recv()
    x_src[...] = p_part[:, mine, :] + c_recv[...]

    def send_plane(j, carry):
        x, y = plane_peer(j)
        remote(x_src.at[y * 4 + x], x_recv.at[j], 1, device(x, y, mz, mc)).start()
        return carry

    lax.fori_loop(1, 16, send_plane, 0)
    plane_all = remote(x_src.at[pl.ds(1, 15)], x_recv.at[pl.ds(1, 15)], 1, partner)

    for s in range(0, width, 512):
        n = min(512, width - s)
        merged_ref[:, s : s + n] = dot_nn(gv[...], av[:, s : s + n]) + ev[:, s : s + n].astype(F32)

    plane_all.wait_recv()
    total = x_src[me]
    for j in range(1, 16):
        total = total + x_recv[j]
    z_buf[mz] = total

    def send_z(j, carry):
        remote(z_buf.at[mz], z_buf.at[mz], 2, device(mx, my, (mz + j) % 8, mc)).start()
        return carry

    lax.fori_loop(1, 8, send_z, 0)
    z_all = remote(z_buf.at[pl.ds(0, 7)], z_buf.at[pl.ds(0, 7)], 2, partner)
    z_all.wait_recv()
    total = z_buf[0]
    for j in range(1, 8):
        total = total + z_buf[j]
    p_full[me, mine, :] = total

    def send_gather(j, carry):
        x, y = plane_peer(j)
        remote(p_full.at[me, mine, :], p_full.at[me, mine, :], 3, device(x, y, mz, mc)).start()
        return carry

    lax.fori_loop(1, 16, send_gather, 0)
    gather_all = remote(x_recv.at[pl.ds(1, 15)], x_recv.at[pl.ds(1, 15)], 3, partner)
    gather_all.wait_recv()
    pair = remote(p_full.at[:, mine, :], p_full.at[:, mine, :], 4, partner)
    pair.start()
    pair.wait_recv()

    for b in range(BLOCKS):
        ps[:, b * LANES : (b + 1) * LANES] = split3(p_full[b])
    pas = split3(fold3(dot_nt(ps[...], av[...])))
    wt = fold3(dot_nt(ps[...], ev[...]) + dot_nt(pas, gv[...]))
    for g in range(4):
        w_src[g] = wt[8 * g : 8 * g + 8, :]

    group = mxh * 2 + mc

    def send_group(j, carry):
        xh, c = group_peer(j)
        remote(w_src.at[xh * 2 + c], w_recv.at[j], 5, device(xh * 2 + mxl, my, mz, c)).start()
        return carry

    lax.fori_loop(1, 4, send_group, 0)
    group_all = remote(w_src.at[pl.ds(1, 3)], w_recv.at[pl.ds(1, 3)], 5, partner)

    p_rows = jnp.concatenate([p_full[b] for b in range(BLOCKS)], axis=1)
    basis_f[...] = p_rows
    gram = dot_nt(p_rows, p_rows, lax.Precision.HIGHEST)

    group_all.wait_recv()
    w_z[mz] = w_src[group] + w_recv[1] + w_recv[2] + w_recv[3]

    def send_wz(j, carry):
        remote(w_z.at[mz], w_z.at[mz], 6, device(mx, my, (mz + j) % 8, mc)).start()
        return carry

    lax.fori_loop(1, 8, send_wz, 0)
    wz_all = remote(w_z.at[pl.ds(0, 7)], w_z.at[pl.ds(0, 7)], 6, partner)

    inverse = inverse_factor(gram)

    wz_all.wait_recv()
    total = w_z[0]
    for j in range(1, 8):
        total = total + w_z[j]
    w_full[group] = total

    def send_wg(j, carry):
        xh, c = group_peer(j)
        remote(w_full.at[group], w_full.at[group], 7, device(xh * 2 + mxl, my, mz, c)).start()
        return carry

    lax.fori_loop(1, 4, send_wg, 0)
    wg_all = remote(w_recv.at[pl.ds(1, 3)], w_recv.at[pl.ds(1, 3)], 7, partner)

    basis = jnp.dot(inverse, basis_f[...], precision=lax.Precision.HIGHEST, preferred_element_type=F32)
    basis_f[...] = basis
    high = basis[:, :width].astype(BF16)
    low = (basis[:, :width] - high.astype(F32)).astype(BF16)
    basis3_ref[...] = jnp.concatenate([high, low, high], axis=0)
    start = dp * share
    base = pl.multiple_of((start // 128) * 128, 128)
    window = basis_f[:, pl.ds(base, 256)]
    pb_ref[...] = pltpu.roll(window, (256 - start % 128) % 256, 1)[:, :share]

    wg_all.wait_recv()
    w_rows = jnp.concatenate([w_full[g] for g in range(4)], axis=0)
    qt = jnp.dot(inverse, w_rows, precision=lax.Precision.HIGHEST, preferred_element_type=F32) * (1.0 / 32)
    qt_ref[...] = qt
    q = qt.T
    q_high = q.astype(BF16)
    q_low = (q - q_high.astype(F32)).astype(BF16)
    q3_ref[...] = jnp.concatenate([q_high, q_high, q_low], axis=1)

    swap.wait_send()
    plane_all.wait_send()
    z_all.wait_send()
    gather_all.wait_send()
    pair.wait_send()
    group_all.wait_send()
    wz_all.wait_send()
    wg_all.wait_send()


def error_kernel(merged_ref, basis3_ref, q3_ref, qt_ref, pb_ref, out_hbm, qt_out, pb_out, stage, sem):
    rows, width = merged_ref.shape
    cuts = [(s, min(64, rows - s)) for s in range(0, rows, 64)]
    copies = []
    for i, (s, n) in enumerate(cuts):
        block = merged_ref[s : s + n, :] - dot_nn(q3_ref[s : s + n, :], basis3_ref[...])
        stage[s : s + n, :] = block.astype(BF16)
        cp = pltpu.make_async_copy(stage.at[pl.ds(s, n)], out_hbm.at[pl.ds(s, n)], sem.at[i])
        cp.start()
        copies.append(cp)
    qt_out[...] = qt_ref[...]
    pb_out[...] = pb_ref[...]
    for cp in copies:
        cp.wait()


def body(activations, out_grads, error_memory, q_previous):
    q_t = q_previous.T
    g_t = out_grads.transpose(0, 2, 1)
    e_t = error_memory.T
    rank, columns = q_t.shape
    width = e_t.shape[0 + 1]
    tokens = activations.shape[1]
    share = width // lax.axis_size("dp")
    padded = BLOCKS * LANES
    half = rank // 2
    any_spec = pl.BlockSpec(memory_space=pl.ANY)
    vmem = pl.BlockSpec(memory_space=pltpu.VMEM)
    merged, basis3, q3, qt, pb = pl.pallas_call(
        reduce_kernel,
        out_shape=(
            jax.ShapeDtypeStruct((columns, width), F32),
            jax.ShapeDtypeStruct((3 * rank, width), BF16),
            jax.ShapeDtypeStruct((columns, 3 * rank), BF16),
            jax.ShapeDtypeStruct((rank, columns), F32),
            jax.ShapeDtypeStruct((rank, share), F32),
        ),
        in_specs=[pl.BlockSpec(memory_space=pltpu.HBM)] * 4,
        out_specs=(vmem,) * 5,
        scratch_shapes=[
            pltpu.VMEM((rank, columns), F32),
            pltpu.VMEM((columns, 2 * tokens), BF16),
            pltpu.VMEM((2 * tokens, padded), BF16),
            pltpu.VMEM((columns, padded), BF16),
            pltpu.VMEM((BLOCKS, rank, LANES), F32),
            pltpu.VMEM((BLOCKS, half, LANES), F32),
            pltpu.VMEM((BLOCKS, half, LANES), F32),
            pltpu.VMEM((BLOCKS, half, LANES), F32),
            pltpu.VMEM((8, half, LANES), F32),
            pltpu.VMEM((BLOCKS, rank, LANES), F32),
            pltpu.VMEM((3 * rank, padded), BF16),
            pltpu.VMEM((4, 8, columns), F32),
            pltpu.VMEM((4, 8, columns), F32),
            pltpu.VMEM((8, 8, columns), F32),
            pltpu.VMEM((4, 8, columns), F32),
            pltpu.VMEM((rank, padded), F32),
            pltpu.SemaphoreType.DMA((16,)),
            pltpu.SemaphoreType.DMA((8,)),
            pltpu.SemaphoreType.DMA((8,)),
        ],
        compiler_params=pltpu.CompilerParams(
            collective_id=0, has_side_effects=True, vmem_limit_bytes=28 << 20
        ),
        name="reduce_kernel",
    )(*[pltpu.with_memory_space_constraint(x, pltpu.HBM) for x in (q_t, g_t, activations, e_t)])
    new_t, q_out, pb_out = pl.pallas_call(
        error_kernel,
        out_shape=(
            jax.ShapeDtypeStruct((columns, width), BF16),
            jax.ShapeDtypeStruct((rank, columns), F32),
            jax.ShapeDtypeStruct((rank, share), F32),
        ),
        in_specs=[vmem] * 5,
        out_specs=(any_spec, vmem, vmem),
        scratch_shapes=[pltpu.VMEM((columns, width), BF16), pltpu.SemaphoreType.DMA((8,))],
        compiler_params=pltpu.CompilerParams(vmem_limit_bytes=20 << 20),
        name="error_kernel",
    )(merged, basis3, q3, qt, pb)
    return new_t.T, pb_out.T, q_out.T


def solution(mesh):
    in_specs = (P(None, "dp", None), P(None, "dp", "mp"), P("dp", "mp"), P("mp", None))
    out_specs = (P("dp", "mp"), P("dp", None), P("mp", None))
    return jax.shard_map(body, mesh=mesh, in_specs=in_specs, out_specs=out_specs, check_vma=False)
```

```python
import functools

import jax
import jax.numpy as jnp
from jax import lax
from jax.experimental import pallas as pl
from jax.experimental.pallas import tpu as pltpu
from jax.sharding import PartitionSpec as P

MESH = pl.DeviceIdType.MESH
F32 = jnp.float32
BF16 = jnp.bfloat16
BLOCKS = 16
LANES = 256
ROW_ORDER = (2, 3, 1, 0)
X_ORDER = (2, 3, 1, 0)
Z_ORDER = (4, 3, 5, 2, 6, 1, 7)
PLANE_FAR_FIRST = sorted(
    ((dx, dy) for dx in range(4) for dy in range(4) if dx + dy),
    key=lambda d: -(min(d[0], 4 - d[0]) + min(d[1], 4 - d[1])),
)
LAG = 3


def split3(x):
    high = x.astype(BF16)
    rest = x - high.astype(F32)
    middle = rest.astype(BF16)
    low = (rest - middle.astype(F32)).astype(BF16)
    return jnp.concatenate([high, middle, low], axis=0)


def fold3(x):
    rows = x.shape[0] // 3
    return x[:rows] + x[rows : 2 * rows] + x[2 * rows :]


def dot_nn(a, b):
    return lax.dot_general(a, b, (((1,), (0,)), ((), ())), preferred_element_type=F32)


def dot_nt(a, b, precision=None):
    return lax.dot_general(
        a, b, (((1,), (1,)), ((), ())), preferred_element_type=F32, precision=precision
    )


def inverse_factor(gram):
    n = gram.shape[0]
    rows = lax.broadcasted_iota(jnp.int32, (n, 2 * n), 0)
    columns = lax.broadcasted_iota(jnp.int32, (n, 2 * n), 1)
    identity = jnp.where(rows + n == columns, 1.0, 0.0).astype(F32)
    wide = jnp.where(columns < n, jnp.concatenate([gram, gram], axis=1), identity)
    row_index = lax.broadcasted_iota(jnp.int32, (n, 1), 0)
    for j in range(n):
        pivot = wide[j : j + 1, j : j + 1]
        scale = lax.rsqrt(pivot)
        scale = scale * (1.5 - 0.5 * pivot * scale * scale)
        row = wide[j : j + 1, :] * scale
        factor = wide[:, j : j + 1] * scale
        below = wide - factor * row
        wide = jnp.where(row_index > j, below, jnp.where(row_index == j, row, wide))
    return wide[:, n:]


def reduce_kernel(
    q_hbm, g_hbm, a_hbm, e_hbm,
    merged_ref, basis3_ref, q3_ref, qt_ref, pb_ref,
    qv, gv, av, ev,
    p_part, c_recv, x_src, x_recv, z_buf, p_full, acc,
    w_src, w_recv, w_z, w_full, basis_f,
    load_sem, ssem, rsem,
):
    rank = qv.shape[0]
    half = rank // 2
    width = e_hbm.shape[1]
    share = pb_ref.shape[1]
    dp, mp = lax.axis_index("dp"), lax.axis_index("mp")
    mz, mxh, mc = dp // 4, (dp // 2) % 2, dp % 2
    my, mxl = mp // 2, mp % 2
    mx = mxh * 2 + mxl
    me = my * 4 + mx

    def device(x, y, z, c):
        return ((z * 2 + x // 2) * 2 + c, y * 2 + x % 2)

    def plane_peer(j):
        return (mx + j % 4) % 4, (my + j // 4) % 4

    def group_peer(j):
        return (mxh + j // 2) % 2, (mc + j % 2) % 2

    partner = device(mx, my, mz, (mc + 1) % 2)

    tokens = a_hbm.shape[1]
    padded = ev.shape[1]
    loads = [pltpu.make_async_copy(q_hbm, qv, load_sem.at[0])]
    loads[0].start()
    g_loads = []
    for m in range(2):
        cp = pltpu.make_async_copy(g_hbm.at[m], gv.at[:, pl.ds(m * tokens, tokens)], load_sem.at[1 + m])
        cp.start()
        g_loads.append(cp)
    step = padded // 4
    short = width - 3 * step
    pieces = []
    for i, dy in enumerate(ROW_ORDER):
        row = (my + dy) % 4
        start = pl.multiple_of(row * step, step)

        def piece_copies(n, start=start, i=i):
            lanes = pl.ds(start, n)
            copies = [
                pltpu.make_async_copy(
                    a_hbm.at[m, :, lanes], av.at[pl.ds(m * tokens, tokens), lanes], load_sem.at[3 + 3 * i + m]
                )
                for m in range(2)
            ]
            copies.append(pltpu.make_async_copy(e_hbm.at[:, lanes], ev.at[:, lanes], load_sem.at[5 + 3 * i]))
            return copies

        def each(action, row=row, piece_copies=piece_copies):
            @pl.when(row < 3)
            def _():
                for cp in piece_copies(step):
                    action(cp)

            @pl.when(row == 3)
            def _():
                for cp in piece_copies(short):
                    action(cp)

        each(lambda cp: cp.start())
        pieces.append((dy, row, start, each))

    barrier = pltpu.get_barrier_semaphore()

    def greet(target):
        pl.semaphore_signal(barrier, inc=1, device_id=target, device_id_type=MESH)

    greet(partner)

    def greet_plane(j, carry):
        x, y = plane_peer(j)
        greet(device(x, y, mz, mc))
        return carry

    lax.fori_loop(1, 16, greet_plane, 0)

    def greet_z(j, carry):
        greet(device(mx, my, (mz + j) % 8, mc))
        return carry

    lax.fori_loop(1, 8, greet_z, 0)
    greet(device(((mxh + 1) % 2) * 2 + mxl, my, mz, (mc + 1) % 2))

    ev[:, width:] = jnp.zeros((ev.shape[0], padded - width), BF16)
    av[:, width:] = jnp.zeros((av.shape[0], padded - width), BF16)

    loads[0].wait()
    qs = split3(qv[...])
    for cp in g_loads:
        cp.wait()
    gqs = split3(fold3(dot_nn(qs, gv[...])))

    def remote(src, dst, send, recv, target):
        return pltpu.make_async_remote_copy(
            src_ref=src, dst_ref=dst, send_sem=ssem.at[send], recv_sem=rsem.at[recv],
            device_id=target, device_id_type=MESH,
        )

    mine = pl.ds(pl.multiple_of(mc * half, half), half)
    other = pl.ds(pl.multiple_of(((mc + 1) % 2) * half, half), half)
    swaps = []

    def to_plane(i):
        dy, row, _, _ = pieces[i]
        four = pl.ds(row * 4, 4)
        swaps[i].wait_recv()
        x_src[four] = p_part[four, mine, :] + c_recv[four]
        for dx in X_ORDER:
            if dx + dy > 0:
                x = (mx + dx) % 4
                remote(x_src.at[row * 4 + x], x_recv.at[dy * 4 + dx], 1, 1, device(x, row, mz, mc)).start()

    for i, (dy, row, start, each) in enumerate(pieces):
        each(lambda cp: cp.wait())
        lanes = pl.ds(start, step)
        r = fold3(dot_nn(qs, ev[:, lanes]) + dot_nn(gqs, av[:, lanes]))
        for b in range(4):
            p_part[row * 4 + b] = r[:, b * LANES : (b + 1) * LANES]
        if i == 0:
            pl.semaphore_wait(barrier, 24)
        four = pl.ds(row * 4, 4)
        swaps.append(remote(p_part.at[four, other, :], c_recv.at[four], 8 + i, 8 + i, partner))
        swaps[i].start()
        if i > 0:
            to_plane(i - 1)
    to_plane(3)
    plane_all = remote(x_src.at[pl.ds(1, 15)], x_recv.at[pl.ds(1, 15)], 1, 1, partner)

    for s in range(0, width, 512):
        n = min(512, width - s)
        merged_ref[:, s : s + n] = dot_nn(gv[...], av[:, s : s + n]) + ev[:, s : s + n].astype(F32)

    plane_all.wait_recv()
    total = x_src[me]
    for j in range(1, 16):
        total = total + x_recv[j]
    z_buf[mz] = total

    for dz in Z_ORDER:
        remote(z_buf.at[mz], z_buf.at[mz], 2, 2, device(mx, my, (mz + dz) % 8, mc)).start()
    z_all = remote(z_buf.at[pl.ds(0, 7)], z_buf.at[pl.ds(0, 7)], 2, 2, partner)
    acc[...] = jnp.zeros_like(acc)
    z_all.wait_recv()
    total = z_buf[0]
    for j in range(1, 8):
        total = total + z_buf[j]
    p_full[me, mine, :] = total

    def block_copy(k, recv, target):
        return remote(p_full.at[k, mine, :], p_full.at[k, mine, :], 3 if recv < 32 else 4, recv, target)

    for dx, dy in PLANE_FAR_FIRST:
        block_copy(me, 16 + dy * 4 + dx, device((mx + dx) % 4, (my + dy) % 4, mz, mc)).start()
    block_copy(me, 32, partner).start()

    def use(k):
        rows = split3(p_full[k])
        lanes = pl.ds(pl.multiple_of(k * LANES, LANES), LANES)
        acc[:, : ev.shape[0]] += fold3(dot_nt(rows, ev[:, lanes]))
        acc[:, 512:] += fold3(dot_nt(rows, av[:, lanes]))

    order = PLANE_FAR_FIRST[::-1]
    sources = [((my - dy) % 4) * 4 + (mx - dx) % 4 for dx, dy in order]
    for n in range(len(order) + LAG):
        if n < len(order):
            dx, dy = order[n]
            block_copy(sources[n], 16 + dy * 4 + dx, partner).wait_recv()
            block_copy(sources[n], 33 + n, partner).start()
        if n == 0:
            block_copy(me, 32, partner).wait_recv()
            use(me)
        if n >= LAG:
            k = n - LAG
            block_copy(sources[k], 33 + k, partner).wait_recv()
            use(sources[k])
    pas = split3(acc[:, 512:])
    wt = acc[:, : ev.shape[0]] + fold3(dot_nt(pas, gv[...]))
    for g in range(4):
        w_src[g] = wt[8 * g : 8 * g + 8, :]
    gather_all = remote(x_recv.at[pl.ds(1, 15)], x_recv.at[pl.ds(1, 15)], 3, 3, partner)
    pair = remote(p_full.at[:, mine, :], p_full.at[:, mine, :], 4, 4, partner)

    group = mxh * 2 + mc

    for j in (2, 3, 1):
        xh, c = group_peer(j)
        remote(w_src.at[xh * 2 + c], w_recv.at[j], 5, 5, device(xh * 2 + mxl, my, mz, c)).start()
    group_all = remote(w_src.at[pl.ds(1, 3)], w_recv.at[pl.ds(1, 3)], 5, 5, partner)

    p_rows = jnp.concatenate([p_full[b] for b in range(BLOCKS)], axis=1)
    basis_f[...] = p_rows
    gram = dot_nt(p_rows, p_rows, lax.Precision.HIGHEST)

    group_all.wait_recv()
    w_z[mz] = w_src[group] + w_recv[1] + w_recv[2] + w_recv[3]

    for dz in Z_ORDER:
        remote(w_z.at[mz], w_z.at[mz], 6, 6, device(mx, my, (mz + dz) % 8, mc)).start()
    wz_all = remote(w_z.at[pl.ds(0, 7)], w_z.at[pl.ds(0, 7)], 6, 6, partner)

    inverse = inverse_factor(gram)

    wz_all.wait_recv()
    total = w_z[0]
    for j in range(1, 8):
        total = total + w_z[j]
    w_full[group] = total

    for j in (2, 3, 1):
        xh, c = group_peer(j)
        remote(w_full.at[group], w_full.at[group], 7, 7, device(xh * 2 + mxl, my, mz, c)).start()
    wg_all = remote(w_recv.at[pl.ds(1, 3)], w_recv.at[pl.ds(1, 3)], 7, 7, partner)

    basis = jnp.dot(inverse, basis_f[...], precision=lax.Precision.HIGHEST, preferred_element_type=F32)
    basis_f[...] = basis
    high = basis[:, :width].astype(BF16)
    low = (basis[:, :width] - high.astype(F32)).astype(BF16)
    basis3_ref[...] = jnp.concatenate([high, low, high], axis=0)
    start = dp * share
    base = pl.multiple_of((start // 128) * 128, 128)
    window = basis_f[:, pl.ds(base, 256)]
    pb_ref[...] = pltpu.roll(window, (256 - start % 128) % 256, 1)[:, :share]

    wg_all.wait_recv()
    w_rows = jnp.concatenate([w_full[g] for g in range(4)], axis=0)
    qt = jnp.dot(inverse, w_rows, precision=lax.Precision.HIGHEST, preferred_element_type=F32) * (1.0 / 32)
    qt_ref[...] = qt
    q = qt.T
    q_high = q.astype(BF16)
    q_low = (q - q_high.astype(F32)).astype(BF16)
    q3_ref[...] = jnp.concatenate([q_high, q_high, q_low], axis=1)

    for swap in swaps:
        swap.wait_send()
    plane_all.wait_send()
    z_all.wait_send()
    gather_all.wait_send()
    pair.wait_send()
    group_all.wait_send()
    wz_all.wait_send()
    wg_all.wait_send()


def error_kernel(merged_ref, basis3_ref, q3_ref, qt_ref, pb_ref, out_hbm, qt_out, pb_out, stage, sem):
    rows, width = merged_ref.shape
    cuts = [(s, min(64, rows - s)) for s in range(0, rows, 64)]
    copies = []
    for i, (s, n) in enumerate(cuts):
        block = merged_ref[s : s + n, :] - dot_nn(q3_ref[s : s + n, :], basis3_ref[...])
        stage[s : s + n, :] = block.astype(BF16)
        cp = pltpu.make_async_copy(stage.at[pl.ds(s, n)], out_hbm.at[pl.ds(s, n)], sem.at[i])
        cp.start()
        copies.append(cp)
    qt_out[...] = qt_ref[...]
    pb_out[...] = pb_ref[...]
    for cp in copies:
        cp.wait()


def body(activations, out_grads, error_memory, q_previous):
    q_t = q_previous.T
    g_t = out_grads.transpose(0, 2, 1)
    e_t = error_memory.T
    rank, columns = q_t.shape
    width = e_t.shape[0 + 1]
    tokens = activations.shape[1]
    share = width // lax.axis_size("dp")
    padded = BLOCKS * LANES
    half = rank // 2
    any_spec = pl.BlockSpec(memory_space=pl.ANY)
    vmem = pl.BlockSpec(memory_space=pltpu.VMEM)
    merged, basis3, q3, qt, pb = pl.pallas_call(
        reduce_kernel,
        out_shape=(
            jax.ShapeDtypeStruct((columns, width), F32),
            jax.ShapeDtypeStruct((3 * rank, width), BF16),
            jax.ShapeDtypeStruct((columns, 3 * rank), BF16),
            jax.ShapeDtypeStruct((rank, columns), F32),
            jax.ShapeDtypeStruct((rank, share), F32),
        ),
        in_specs=[pl.BlockSpec(memory_space=pltpu.HBM)] * 4,
        out_specs=(vmem,) * 5,
        scratch_shapes=[
            pltpu.VMEM((rank, columns), F32),
            pltpu.VMEM((columns, 2 * tokens), BF16),
            pltpu.VMEM((2 * tokens, padded), BF16),
            pltpu.VMEM((columns, padded), BF16),
            pltpu.VMEM((BLOCKS, rank, LANES), F32),
            pltpu.VMEM((BLOCKS, half, LANES), F32),
            pltpu.VMEM((BLOCKS, half, LANES), F32),
            pltpu.VMEM((BLOCKS, half, LANES), F32),
            pltpu.VMEM((8, half, LANES), F32),
            pltpu.VMEM((BLOCKS, rank, LANES), F32),
            pltpu.VMEM((rank, 512 + 2 * tokens), F32),
            pltpu.VMEM((4, 8, columns), F32),
            pltpu.VMEM((4, 8, columns), F32),
            pltpu.VMEM((8, 8, columns), F32),
            pltpu.VMEM((4, 8, columns), F32),
            pltpu.VMEM((rank, padded), F32),
            pltpu.SemaphoreType.DMA((16,)),
            pltpu.SemaphoreType.DMA((12,)),
            pltpu.SemaphoreType.DMA((48,)),
        ],
        compiler_params=pltpu.CompilerParams(
            collective_id=0, has_side_effects=True, vmem_limit_bytes=28 << 20
        ),
        name="reduce_kernel",
    )(*[pltpu.with_memory_space_constraint(x, pltpu.HBM) for x in (q_t, g_t, activations, e_t)])
    new_t, q_out, pb_out = pl.pallas_call(
        error_kernel,
        out_shape=(
            jax.ShapeDtypeStruct((columns, width), BF16),
            jax.ShapeDtypeStruct((rank, columns), F32),
            jax.ShapeDtypeStruct((rank, share), F32),
        ),
        in_specs=[vmem] * 5,
        out_specs=(any_spec, vmem, vmem),
        scratch_shapes=[pltpu.VMEM((columns, width), BF16), pltpu.SemaphoreType.DMA((8,))],
        compiler_params=pltpu.CompilerParams(vmem_limit_bytes=20 << 20),
        name="error_kernel",
    )(merged, basis3, q3, qt, pb)
    return new_t.T, pb_out.T, q_out.T


def solution(mesh):
    in_specs = (P(None, "dp", None), P(None, "dp", "mp"), P("dp", "mp"), P("mp", None))
    out_specs = (P("dp", "mp"), P("dp", None), P("mp", None))
    return jax.shard_map(body, mesh=mesh, in_specs=in_specs, out_specs=out_specs, check_vma=False)
```

```python
import functools

import jax
import jax.numpy as jnp
from jax import lax
from jax.experimental import pallas as pl
from jax.experimental.pallas import tpu as pltpu
from jax.sharding import PartitionSpec as P

MESH = pl.DeviceIdType.MESH
F32 = jnp.float32
BF16 = jnp.bfloat16
BLOCKS = 16
LANES = 256
ROW_ORDER = (2, 3, 1, 0)
X_ORDER = (2, 3, 1, 0)
Z_ORDER = (4, 3, 5, 2, 6, 1, 7)


def hops(step):
    return sum(min(d, 4 - d) for d in step)


SEND_ORDER = sorted(
    ((dx, dy) for dx in range(4) for dy in range(4) if dx + dy), key=lambda step: (4, 2, 3, 1, 0)[hops(step)]
)


def split3(x):
    high = x.astype(BF16)
    rest = x - high.astype(F32)
    middle = rest.astype(BF16)
    low = (rest - middle.astype(F32)).astype(BF16)
    return jnp.concatenate([high, middle, low], axis=0)


def fold3(x):
    rows = x.shape[0] // 3
    return x[:rows] + x[rows : 2 * rows] + x[2 * rows :]


def dot_nn(a, b):
    return lax.dot_general(a, b, (((1,), (0,)), ((), ())), preferred_element_type=F32)


def dot_nt(a, b, precision=None):
    return lax.dot_general(
        a, b, (((1,), (1,)), ((), ())), preferred_element_type=F32, precision=precision
    )


def inverse_factor(gram):
    n = gram.shape[0]
    rows = lax.broadcasted_iota(jnp.int32, (n, 2 * n), 0)
    columns = lax.broadcasted_iota(jnp.int32, (n, 2 * n), 1)
    identity = jnp.where(rows + n == columns, 1.0, 0.0).astype(F32)
    wide = jnp.where(columns < n, jnp.concatenate([gram, gram], axis=1), identity)
    row_index = lax.broadcasted_iota(jnp.int32, (n, 1), 0)
    for j in range(n):
        pivot = wide[j : j + 1, j : j + 1]
        scale = lax.rsqrt(pivot)
        scale = scale * (1.5 - 0.5 * pivot * scale * scale)
        row = wide[j : j + 1, :] * scale
        factor = wide[:, j : j + 1] * scale
        below = wide - factor * row
        wide = jnp.where(row_index > j, below, jnp.where(row_index == j, row, wide))
    return wide[:, n:]


def reduce_kernel(
    q_hbm, g_hbm, a_hbm, e_hbm,
    merged_ref, basis3_ref, q3_ref, qt_ref, pb_ref,
    qv, gv, av, ev,
    p_part, c_recv, x_src, x_recv, z_buf, p_full, w_acc, a_acc, inv_s,
    w_src, w_recv, w_z, w_full, basis_f,
    load_sem, ssem, rsem,
):
    rank = qv.shape[0]
    half = rank // 2
    width = e_hbm.shape[1]
    share = pb_ref.shape[1]
    dp, mp = lax.axis_index("dp"), lax.axis_index("mp")
    mz, mxh, mc = dp // 4, (dp // 2) % 2, dp % 2
    my, mxl = mp // 2, mp % 2
    mx = mxh * 2 + mxl
    me = my * 4 + mx

    def device(x, y, z, c):
        return ((z * 2 + x // 2) * 2 + c, y * 2 + x % 2)

    def plane_peer(j):
        return (mx + j % 4) % 4, (my + j // 4) % 4

    def group_peer(j):
        return (mxh + j // 2) % 2, (mc + j % 2) % 2

    partner = device(mx, my, mz, (mc + 1) % 2)

    tokens = a_hbm.shape[1]
    padded = ev.shape[1]
    loads = [pltpu.make_async_copy(q_hbm, qv, load_sem.at[0])]
    loads[0].start()
    g_loads = []
    for m in range(2):
        cp = pltpu.make_async_copy(g_hbm.at[m], gv.at[:, pl.ds(m * tokens, tokens)], load_sem.at[1 + m])
        cp.start()
        g_loads.append(cp)
    step = padded // 4
    short = width - 3 * step
    pieces = []
    for i, dy in enumerate(ROW_ORDER):
        row = (my + dy) % 4
        start = pl.multiple_of(row * step, step)

        def piece_copies(n, start=start, i=i):
            lanes = pl.ds(start, n)
            copies = [
                pltpu.make_async_copy(
                    a_hbm.at[m, :, lanes], av.at[pl.ds(m * tokens, tokens), lanes], load_sem.at[3 + 3 * i + m]
                )
                for m in range(2)
            ]
            copies.append(pltpu.make_async_copy(e_hbm.at[:, lanes], ev.at[:, lanes], load_sem.at[5 + 3 * i]))
            return copies

        def each(action, row=row, piece_copies=piece_copies):
            @pl.when(row < 3)
            def _():
                for cp in piece_copies(step):
                    action(cp)

            @pl.when(row == 3)
            def _():
                for cp in piece_copies(short):
                    action(cp)

        each(lambda cp: cp.start())
        pieces.append((dy, row, start, each))

    barrier = pltpu.get_barrier_semaphore()

    def greet(target):
        pl.semaphore_signal(barrier, inc=1, device_id=target, device_id_type=MESH)

    greet(partner)

    def greet_plane(j, carry):
        x, y = plane_peer(j)
        greet(device(x, y, mz, mc))
        return carry

    lax.fori_loop(1, 16, greet_plane, 0)

    def greet_z(j, carry):
        greet(device(mx, my, (mz + j) % 8, mc))
        return carry

    lax.fori_loop(1, 8, greet_z, 0)
    greet(device(((mxh + 1) % 2) * 2 + mxl, my, mz, (mc + 1) % 2))

    ev[:, width:] = jnp.zeros((ev.shape[0], padded - width), BF16)
    av[:, width:] = jnp.zeros((av.shape[0], padded - width), BF16)

    loads[0].wait()
    qs = split3(qv[...])
    for cp in g_loads:
        cp.wait()
    gqs = split3(fold3(dot_nn(qs, gv[...])))

    def remote(src, dst, send, recv, target):
        return pltpu.make_async_remote_copy(
            src_ref=src, dst_ref=dst, send_sem=ssem.at[send], recv_sem=rsem.at[recv],
            device_id=target, device_id_type=MESH,
        )

    mine = pl.ds(pl.multiple_of(mc * half, half), half)
    other = pl.ds(pl.multiple_of(((mc + 1) % 2) * half, half), half)
    swaps = []

    def to_plane(i):
        dy, row, _, _ = pieces[i]
        four = pl.ds(row * 4, 4)
        swaps[i].wait_recv()
        x_src[four] = p_part[four, mine, :] + c_recv[four]
        for dx in X_ORDER:
            if dx + dy > 0:
                x = (mx + dx) % 4
                remote(x_src.at[row * 4 + x], x_recv.at[dy * 4 + dx], 1, 1, device(x, row, mz, mc)).start()

    for i, (dy, row, start, each) in enumerate(pieces):
        each(lambda cp: cp.wait())
        lanes = pl.ds(start, step)
        r = fold3(dot_nn(qs, ev[:, lanes]) + dot_nn(gqs, av[:, lanes]))
        for b in range(4):
            p_part[row * 4 + b] = r[:, b * LANES : (b + 1) * LANES]
    pl.semaphore_wait(barrier, 24)
    for i, (dy, row, start, each) in enumerate(pieces):
        four = pl.ds(row * 4, 4)
        swaps.append(remote(p_part.at[four, other, :], c_recv.at[four], 8 + i, 8 + i, partner))
        swaps[i].start()
    for i in range(3):
        to_plane(i)
    to_plane(3)
    plane_all = remote(x_src.at[pl.ds(1, 15)], x_recv.at[pl.ds(1, 15)], 1, 1, partner)

    for s in range(0, width, 512):
        n = min(512, width - s)
        merged_ref[:, s : s + n] = dot_nn(gv[...], av[:, s : s + n]) + ev[:, s : s + n].astype(F32)

    plane_all.wait_recv()
    total = x_src[me]
    for j in range(1, 16):
        total = total + x_recv[j]
    z_buf[mz] = total

    for dz in Z_ORDER:
        remote(z_buf.at[mz], z_buf.at[mz], 2, 2, device(mx, my, (mz + dz) % 8, mc)).start()
    z_all = remote(z_buf.at[pl.ds(0, 7)], z_buf.at[pl.ds(0, 7)], 2, 2, partner)
    z_all.wait_recv()
    total = z_buf[0]
    for j in range(1, 8):
        total = total + z_buf[j]
    p_full[me, mine, :] = total

    def block_copy(k, recv, target):
        return remote(p_full.at[k, mine, :], p_full.at[k, mine, :], 3 if recv < 32 else 4, recv, target)

    for dx, dy in SEND_ORDER:
        block_copy(me, 16 + dy * 4 + dx, device((mx + dx) % 4, (my + dy) % 4, mz, mc)).start()
    block_copy(me, 32, partner).start()

    def use(group):
        w_sum, a_sum = None, None
        for k, recv in group:
            block_copy(k, recv, partner).wait_recv()
        for k, recv in group:
            rows = split3(p_full[k])
            lanes = pl.ds(pl.multiple_of(k * LANES, LANES), LANES)
            w_part = dot_nt(ev[:, lanes], rows)
            a_part = dot_nt(av[:, lanes], rows)
            w_sum = w_part if w_sum is None else w_sum + w_part
            a_sum = a_part if a_sum is None else a_sum + a_part
        return w_sum, a_sum

    waiting = [(me, 32)]
    for n, distances in enumerate(((1,), (2,), (3, 4))):
        arrived = []
        for dx, dy in SEND_ORDER:
            if hops((dx, dy)) in distances:
                k = ((my - dy) % 4) * 4 + (mx - dx) % 4
                block_copy(k, 16 + dy * 4 + dx, partner).wait_recv()
                block_copy(k, 32 + dy * 4 + dx, partner).start()
                arrived.append((k, 32 + dy * 4 + dx))
        if n > 0:
            w_sum, a_sum = use(waiting)
            w_acc[...] = w_sum if n == 1 else w_acc[...] + w_sum
            a_acc[...] = a_sum if n == 1 else a_acc[...] + a_sum
            waiting = []
        waiting = waiting + arrived
    w_sum, a_sum = use(waiting)
    pas = split3(fold3((a_acc[...] + a_sum).T))
    wt = fold3((w_acc[...] + w_sum + dot_nt(gv[...], pas)).T)
    for g in range(4):
        w_src[g] = wt[8 * g : 8 * g + 8, :]
    gather_all = remote(x_recv.at[pl.ds(1, 15)], x_recv.at[pl.ds(1, 15)], 3, 3, partner)
    pair = remote(p_full.at[:, mine, :], p_full.at[:, mine, :], 4, 4, partner)

    group = mxh * 2 + mc

    for j in (2, 3, 1):
        xh, c = group_peer(j)
        remote(w_src.at[xh * 2 + c], w_recv.at[j], 5, 5, device(xh * 2 + mxl, my, mz, c)).start()
    group_all = remote(w_src.at[pl.ds(1, 3)], w_recv.at[pl.ds(1, 3)], 5, 5, partner)

    p_rows = jnp.concatenate([p_full[b] for b in range(BLOCKS)], axis=1)
    basis_f[...] = p_rows
    inv_s[...] = dot_nt(p_rows, p_rows, lax.Precision.HIGHEST)

    group_all.wait_recv()
    w_z[mz] = w_src[group] + w_recv[1] + w_recv[2] + w_recv[3]

    for dz in Z_ORDER:
        remote(w_z.at[mz], w_z.at[mz], 6, 6, device(mx, my, (mz + dz) % 8, mc)).start()
    wz_all = remote(w_z.at[pl.ds(0, 7)], w_z.at[pl.ds(0, 7)], 6, 6, partner)

    inv_s[...] = inverse_factor(inv_s[...])

    wz_all.wait_recv()
    total = w_z[0]
    for j in range(1, 8):
        total = total + w_z[j]
    w_full[group] = total

    for j in (2, 3, 1):
        xh, c = group_peer(j)
        remote(w_full.at[group], w_full.at[group], 7, 7, device(xh * 2 + mxl, my, mz, c)).start()
    wg_all = remote(w_recv.at[pl.ds(1, 3)], w_recv.at[pl.ds(1, 3)], 7, 7, partner)

    inverse = inv_s[...]
    basis = jnp.dot(inverse, basis_f[...], precision=lax.Precision.HIGHEST, preferred_element_type=F32)
    basis_f[...] = basis
    high = basis[:, :width].astype(BF16)
    low = (basis[:, :width] - high.astype(F32)).astype(BF16)
    basis3_ref[...] = jnp.concatenate([high, low, high], axis=0)
    start = dp * share
    base = pl.multiple_of((start // 128) * 128, 128)
    window = basis_f[:, pl.ds(base, 256)]
    pb_ref[...] = pltpu.roll(window, (256 - start % 128) % 256, 1)[:, :share]

    wg_all.wait_recv()
    w_rows = jnp.concatenate([w_full[g] for g in range(4)], axis=0)
    qt = jnp.dot(inverse, w_rows, precision=lax.Precision.HIGHEST, preferred_element_type=F32) * (1.0 / 32)
    qt_ref[...] = qt
    q = qt.T
    q_high = q.astype(BF16)
    q_low = (q - q_high.astype(F32)).astype(BF16)
    q3_ref[...] = jnp.concatenate([q_high, q_high, q_low], axis=1)

    for swap in swaps:
        swap.wait_send()
    plane_all.wait_send()
    z_all.wait_send()
    gather_all.wait_send()
    pair.wait_send()
    group_all.wait_send()
    wz_all.wait_send()
    wg_all.wait_send()


def error_kernel(merged_ref, basis3_ref, q3_ref, qt_ref, pb_ref, out_hbm, qt_out, pb_out, stage, sem):
    rows, width = merged_ref.shape
    cuts = [(s, min(64, rows - s)) for s in range(0, rows, 64)]
    copies = []
    for i, (s, n) in enumerate(cuts):
        block = merged_ref[s : s + n, :] - dot_nn(q3_ref[s : s + n, :], basis3_ref[...])
        stage[s : s + n, :] = block.astype(BF16)
        cp = pltpu.make_async_copy(stage.at[pl.ds(s, n)], out_hbm.at[pl.ds(s, n)], sem.at[i])
        cp.start()
        copies.append(cp)
    qt_out[...] = qt_ref[...]
    pb_out[...] = pb_ref[...]
    for cp in copies:
        cp.wait()


def body(activations, out_grads, error_memory, q_previous):
    q_t = q_previous.T
    g_t = out_grads.transpose(0, 2, 1)
    e_t = error_memory.T
    rank, columns = q_t.shape
    width = e_t.shape[0 + 1]
    tokens = activations.shape[1]
    share = width // lax.axis_size("dp")
    padded = BLOCKS * LANES
    half = rank // 2
    any_spec = pl.BlockSpec(memory_space=pl.ANY)
    vmem = pl.BlockSpec(memory_space=pltpu.VMEM)
    merged, basis3, q3, qt, pb = pl.pallas_call(
        reduce_kernel,
        out_shape=(
            jax.ShapeDtypeStruct((columns, width), F32),
            jax.ShapeDtypeStruct((3 * rank, width), BF16),
            jax.ShapeDtypeStruct((columns, 3 * rank), BF16),
            jax.ShapeDtypeStruct((rank, columns), F32),
            jax.ShapeDtypeStruct((rank, share), F32),
        ),
        in_specs=[pl.BlockSpec(memory_space=pltpu.HBM)] * 4,
        out_specs=(vmem,) * 5,
        scratch_shapes=[
            pltpu.VMEM((rank, columns), F32),
            pltpu.VMEM((columns, 2 * tokens), BF16),
            pltpu.VMEM((2 * tokens, padded), BF16),
            pltpu.VMEM((columns, padded), BF16),
            pltpu.VMEM((BLOCKS, rank, LANES), F32),
            pltpu.VMEM((BLOCKS, half, LANES), F32),
            pltpu.VMEM((BLOCKS, half, LANES), F32),
            pltpu.VMEM((BLOCKS, half, LANES), F32),
            pltpu.VMEM((8, half, LANES), F32),
            pltpu.VMEM((BLOCKS, rank, LANES), F32),
            pltpu.VMEM((columns, 3 * rank), F32),
            pltpu.VMEM((2 * tokens, 3 * rank), F32),
            pltpu.VMEM((rank, rank), F32),
            pltpu.VMEM((4, 8, columns), F32),
            pltpu.VMEM((4, 8, columns), F32),
            pltpu.VMEM((8, 8, columns), F32),
            pltpu.VMEM((4, 8, columns), F32),
            pltpu.VMEM((rank, padded), F32),
            pltpu.SemaphoreType.DMA((16,)),
            pltpu.SemaphoreType.DMA((12,)),
            pltpu.SemaphoreType.DMA((48,)),
        ],
        compiler_params=pltpu.CompilerParams(
            collective_id=0, has_side_effects=True, vmem_limit_bytes=28 << 20
        ),
        name="reduce_kernel",
    )(*[pltpu.with_memory_space_constraint(x, pltpu.HBM) for x in (q_t, g_t, activations, e_t)])
    new_t, q_out, pb_out = pl.pallas_call(
        error_kernel,
        out_shape=(
            jax.ShapeDtypeStruct((columns, width), BF16),
            jax.ShapeDtypeStruct((rank, columns), F32),
            jax.ShapeDtypeStruct((rank, share), F32),
        ),
        in_specs=[vmem] * 5,
        out_specs=(any_spec, vmem, vmem),
        scratch_shapes=[pltpu.VMEM((columns, width), BF16), pltpu.SemaphoreType.DMA((8,))],
        compiler_params=pltpu.CompilerParams(vmem_limit_bytes=20 << 20),
        name="error_kernel",
    )(merged, basis3, q3, qt, pb)
    return new_t.T, pb_out.T, q_out.T


def solution(mesh):
    in_specs = (P(None, "dp", None), P(None, "dp", "mp"), P("dp", "mp"), P("mp", None))
    out_specs = (P("dp", "mp"), P("dp", None), P("mp", None))
    return jax.shard_map(body, mesh=mesh, in_specs=in_specs, out_specs=out_specs, check_vma=False)
```

```python
import functools

import jax
import jax.numpy as jnp
from jax import lax
from jax.experimental import pallas as pl
from jax.experimental.pallas import tpu as pltpu
from jax.sharding import PartitionSpec as P

MESH = pl.DeviceIdType.MESH
F32 = jnp.float32
BF16 = jnp.bfloat16
BLOCKS = 16
LANES = 256
ROW_ORDER = (2, 3, 1, 0)
X_ORDER = (2, 3, 1, 0)
BARRIER_AT = 2
P_PARTS = 2
P_Z_ORDER = (4, 3, 5, 2, 6, 1, 7, 0)
W_Z_ORDER = (0, 1, 2, 3, 4, 5, 6, 7)


def hops(step):
    return sum(min(d, 4 - d) for d in step)


SEND_ORDER = sorted(
    ((dx, dy) for dx in range(4) for dy in range(4) if dx + dy), key=lambda step: (4, 2, 3, 1, 0)[hops(step)]
)


def split_parts(x):
    high = x.astype(BF16)
    rest = x - high.astype(F32)
    middle = rest.astype(BF16)
    return high, middle, (rest - middle.astype(F32)).astype(BF16)


def split3(x):
    return jnp.concatenate(split_parts(x), axis=0)


def factor_terms(x):
    high, middle, low = split_parts(x)
    return jnp.concatenate([high, middle, low, high, middle, high], axis=1)


def rows_terms(y):
    high, middle, low = split_parts(y)
    return jnp.concatenate([high, high, high, middle, middle, low], axis=0)


def fold3(x):
    rows = x.shape[0] // 3
    return x[:rows] + x[rows : 2 * rows] + x[2 * rows :]


def dot_nn(a, b):
    return lax.dot_general(a, b, (((1,), (0,)), ((), ())), preferred_element_type=F32)


def dot_nt(a, b, precision=None):
    return lax.dot_general(
        a, b, (((1,), (1,)), ((), ())), preferred_element_type=F32, precision=precision
    )


def inverse_factor(gram):
    n = gram.shape[0]
    rows = lax.broadcasted_iota(jnp.int32, (n, 2 * n), 0)
    columns = lax.broadcasted_iota(jnp.int32, (n, 2 * n), 1)
    identity = jnp.where(rows + n == columns, 1.0, 0.0).astype(F32)
    wide = jnp.where(columns < n, jnp.concatenate([gram, gram], axis=1), identity)
    row_index = lax.broadcasted_iota(jnp.int32, (n, 1), 0)
    for j in range(n):
        pivot = wide[j : j + 1, j : j + 1]
        scale = lax.rsqrt(pivot)
        scale = scale * (1.5 - 0.5 * pivot * scale * scale)
        row = wide[j : j + 1, :] * scale
        factor = wide[:, j : j + 1] * scale
        below = wide - factor * row
        wide = jnp.where(row_index > j, below, jnp.where(row_index == j, row, wide))
    return wide[:, n:]


def reduce_kernel(
    q_hbm, g_hbm, a_hbm, e_hbm,
    merged_ref, basis3_ref, q3_ref, qt_ref, pb_ref,
    qv, gv, av, ev,
    p_part, c_recv, x_src, x_recv, z_buf, p_full, w_acc, a_acc, inv_s,
    w_src, w_recv, w_z, w_full, basis_f,
    load_sem, ssem, rsem,
):
    rank = qv.shape[0]
    half = rank // 2
    width = e_hbm.shape[1]
    share = pb_ref.shape[1]
    dp, mp = lax.axis_index("dp"), lax.axis_index("mp")
    mz, mxh, mc = dp // 4, (dp // 2) % 2, dp % 2
    my, mxl = mp // 2, mp % 2
    mx = mxh * 2 + mxl
    me = my * 4 + mx

    def device(x, y, z, c):
        return ((z * 2 + x // 2) * 2 + c, y * 2 + x % 2)

    def plane_peer(j):
        return (mx + j % 4) % 4, (my + j // 4) % 4

    def group_peer(j):
        return (mxh + j // 2) % 2, (mc + j % 2) % 2

    partner = device(mx, my, mz, (mc + 1) % 2)

    tokens = a_hbm.shape[1]
    padded = ev.shape[1]
    loads = [pltpu.make_async_copy(q_hbm, qv, load_sem.at[0])]
    loads[0].start()
    g_loads = []
    for m in range(2):
        cp = pltpu.make_async_copy(g_hbm.at[m], gv.at[:, pl.ds(m * tokens, tokens)], load_sem.at[1 + m])
        cp.start()
        g_loads.append(cp)
    step = padded // 4
    short = width - 3 * step
    pieces = []
    for i, dy in enumerate(ROW_ORDER):
        row = (my + dy) % 4
        start = pl.multiple_of(row * step, step)

        def piece_copies(n, start=start, i=i):
            lanes = pl.ds(start, n)
            copies = [
                pltpu.make_async_copy(
                    a_hbm.at[m, :, lanes], av.at[pl.ds(m * tokens, tokens), lanes], load_sem.at[3 + 3 * i + m]
                )
                for m in range(2)
            ]
            copies.append(pltpu.make_async_copy(e_hbm.at[:, lanes], ev.at[:, lanes], load_sem.at[5 + 3 * i]))
            return copies

        def each(action, row=row, piece_copies=piece_copies):
            @pl.when(row < 3)
            def _():
                for cp in piece_copies(step):
                    action(cp)

            @pl.when(row == 3)
            def _():
                for cp in piece_copies(short):
                    action(cp)

        each(lambda cp: cp.start())
        pieces.append((dy, row, start, each))

    barrier = pltpu.get_barrier_semaphore()

    def greet(target):
        pl.semaphore_signal(barrier, inc=1, device_id=target, device_id_type=MESH)

    greet(partner)

    def greet_plane(j, carry):
        x, y = plane_peer(j)
        greet(device(x, y, mz, mc))
        return carry

    lax.fori_loop(1, 16, greet_plane, 0)

    def greet_z(j, carry):
        greet(device(mx, my, (mz + j) % 8, mc))
        return carry

    lax.fori_loop(1, 8, greet_z, 0)
    greet(device(((mxh + 1) % 2) * 2 + mxl, my, mz, (mc + 1) % 2))

    ev[:, width:] = jnp.zeros((ev.shape[0], padded - width), BF16)
    av[:, width:] = jnp.zeros((av.shape[0], padded - width), BF16)

    loads[0].wait()
    qs = split3(qv[...])
    for cp in g_loads:
        cp.wait()
    gqs = split3(fold3(dot_nn(qs, gv[...])))

    def remote(src, dst, send, recv, target):
        return pltpu.make_async_remote_copy(
            src_ref=src, dst_ref=dst, send_sem=ssem.at[send], recv_sem=rsem.at[recv],
            device_id=target, device_id_type=MESH,
        )

    def along_z(order, send):
        for z in order:

            @pl.when(z != mz)
            def _(z=z):
                send(device(mx, my, z, mc))

    mine = pl.ds(pl.multiple_of(mc * half, half), half)
    other = pl.ds(pl.multiple_of(((mc + 1) % 2) * half, half), half)
    swaps = []

    cuts = [pl.ds(h * (half // P_PARTS), half // P_PARTS) for h in range(P_PARTS)]

    def to_plane(i, h):
        dy, row, _, _ = pieces[i]
        for dx in X_ORDER:
            if dx + dy > 0:
                x = (mx + dx) % 4
                remote(
                    x_src.at[row * 4 + x, cuts[h], :], x_recv.at[dy * 4 + dx, cuts[h], :], 1, 12 + h, device(x, row, mz, mc)
                ).start()

    for i, (dy, row, start, each) in enumerate(pieces):
        each(lambda cp: cp.wait())
        lanes = pl.ds(start, step)
        r = fold3(dot_nn(qs, ev[:, lanes]) + dot_nn(gqs, av[:, lanes]))
        for b in range(4):
            p_part[row * 4 + b] = r[:, b * LANES : (b + 1) * LANES]
        four = pl.ds(row * 4, 4)
        swaps.append(remote(p_part.at[four, other, :], c_recv.at[four], 8 + i, 8 + i, partner))
        if i == BARRIER_AT:
            pl.semaphore_wait(barrier, 24)
            for swap in swaps[:i]:
                swap.start()
        if i >= BARRIER_AT:
            swaps[i].start()
    for i, (dy, row, start, each) in enumerate(pieces):
        four = pl.ds(row * 4, 4)
        swaps[i].wait_recv()
        x_src[four] = p_part[four, mine, :] + c_recv[four]
        to_plane(i, 0)
    for h in range(1, P_PARTS):
        for i in range(4):
            to_plane(i, h)
    plane_all = remote(x_src.at[pl.ds(1, 15)], x_recv.at[pl.ds(1, 15)], 1, 1, partner)

    for s in range(0, width, 512):
        n = min(512, width - s)
        merged_ref[:, s : s + n] = dot_nn(gv[...], av[:, s : s + n]) + ev[:, s : s + n].astype(F32)

    for h, cut in enumerate(cuts):
        arrivals = x_recv.at[pl.ds(1, 15), cut, :]
        remote(arrivals, arrivals, 1, 12 + h, partner).wait_recv()
        total = x_src[me, cut, :]
        for j in range(1, 16):
            total = total + x_recv[j, cut, :]
        z_buf[mz, cut, :] = total
        block = z_buf.at[mz, cut, :]
        along_z(P_Z_ORDER, lambda target, block=block, h=h: remote(block, block, 2, 14 + h, target).start())
    z_all = remote(z_buf.at[pl.ds(0, 7)], z_buf.at[pl.ds(0, 7)], 2, 2, partner)
    for h, cut in enumerate(cuts):
        arrivals = z_buf.at[pl.ds(0, 7), cut, :]
        remote(arrivals, arrivals, 2, 14 + h, partner).wait_recv()
        total = z_buf[0, cut, :]
        for j in range(1, 8):
            total = total + z_buf[j, cut, :]
        rows = pl.ds(pl.multiple_of(mc * half + h * (half // P_PARTS), 8), half // P_PARTS)
        p_full[me, rows, :] = total
        block = p_full.at[me, rows, :]
        for dx, dy in SEND_ORDER:
            remote(
                block, block, 3, 16 + dy * 4 + dx, device((mx + dx) % 4, (my + dy) % 4, mz, mc)
            ).start()

    def block_copy(k, recv, target):
        return remote(p_full.at[k, mine, :], p_full.at[k, mine, :], 3 if recv < 32 else 4, recv, target)

    block_copy(me, 32, partner).start()

    def use(group):
        w_sum, a_sum = None, None
        for k, recv in group:
            block_copy(k, recv, partner).wait_recv()
        for k, recv in group:
            rows = split3(p_full[k])
            lanes = pl.ds(pl.multiple_of(k * LANES, LANES), LANES)
            w_part = dot_nt(ev[:, lanes], rows)
            a_part = dot_nt(rows, av[:, lanes])
            w_sum = w_part if w_sum is None else w_sum + w_part
            a_sum = a_part if a_sum is None else a_sum + a_part
        return w_sum, a_sum

    waiting = [(me, 32)]
    for n, distances in enumerate(((1,), (2,), (3, 4))):
        arrived = []
        for dx, dy in SEND_ORDER:
            if hops((dx, dy)) in distances:
                k = ((my - dy) % 4) * 4 + (mx - dx) % 4
                block_copy(k, 16 + dy * 4 + dx, partner).wait_recv()
                block_copy(k, 32 + dy * 4 + dx, partner).start()
                arrived.append((k, 32 + dy * 4 + dx))
        if n > 0:
            w_sum, a_sum = use(waiting)
            w_acc[...] = w_sum if n == 1 else w_acc[...] + w_sum
            a_acc[...] = a_sum if n == 1 else a_acc[...] + a_sum
            waiting = []
        waiting = waiting + arrived
    w_sum, a_sum = use(waiting)
    pas = split3(fold3(a_acc[...] + a_sum))
    wt = fold3((w_acc[...] + w_sum + dot_nt(gv[...], pas)).T)
    for g in range(4):
        w_src[g] = wt[8 * g : 8 * g + 8, :]
    gather_all = remote(x_recv.at[pl.ds(1, 15)], x_recv.at[pl.ds(1, 15)], 3, 3, partner)
    pair = remote(p_full.at[:, mine, :], p_full.at[:, mine, :], 4, 4, partner)

    group = mxh * 2 + mc

    columns = w_src.shape[2]
    strips = [pl.ds(0, columns)]
    for h, strip in enumerate(strips):
        for j in (2, 3, 1):
            xh, c = group_peer(j)
            remote(
                w_src.at[xh * 2 + c, :, strip], w_recv.at[j, :, strip], 5, 5 + 2 * h, device(xh * 2 + mxl, my, mz, c)
            ).start()
    group_all = remote(w_src.at[pl.ds(1, 3)], w_recv.at[pl.ds(1, 3)], 5, 5, partner)

    p_rows = jnp.concatenate([p_full[b] for b in range(BLOCKS)], axis=1)
    basis_f[...] = p_rows
    inv_s[...] = dot_nt(p_rows, p_rows, lax.Precision.HIGHEST)

    for h, strip in enumerate(strips):
        arrivals = w_recv.at[pl.ds(1, 3), :, strip]
        remote(arrivals, arrivals, 5, 5 + 2 * h, partner).wait_recv()
        w_z[mz, :, strip] = w_src[group, :, strip] + w_recv[1, :, strip] + w_recv[2, :, strip] + w_recv[3, :, strip]
        block = w_z.at[mz, :, strip]
        along_z(W_Z_ORDER, lambda target, block=block, h=h: remote(block, block, 6, h, target).start())
    wz_all = remote(w_z.at[pl.ds(0, 7)], w_z.at[pl.ds(0, 7)], 6, 6, partner)

    inv_s[...] = inverse_factor(inv_s[...])

    for h, strip in enumerate(strips):
        arrivals = w_z.at[pl.ds(0, 7), :, strip]
        remote(arrivals, arrivals, 6, h, partner).wait_recv()
        total = w_z[0, :, strip]
        for j in range(1, 8):
            total = total + w_z[j, :, strip]
        w_full[group, :, strip] = total
        block = w_full.at[group, :, strip]
        for j in (2, 3, 1):
            xh, c = group_peer(j)
            remote(block, block, 7, 6, device(xh * 2 + mxl, my, mz, c)).start()
    wg_all = remote(w_recv.at[pl.ds(1, 3)], w_recv.at[pl.ds(1, 3)], 7, 6, partner)

    inverse = inv_s[...]
    inverse_terms = factor_terms(inverse * (1.0 / 32))
    basis = jnp.dot(inverse, basis_f[...], precision=lax.Precision.HIGHEST, preferred_element_type=F32)
    basis_f[...] = basis
    high = basis[:, :width].astype(BF16)
    low = (basis[:, :width] - high.astype(F32)).astype(BF16)
    basis3_ref[...] = jnp.concatenate([high, low, high], axis=0)
    start = dp * share
    base = pl.multiple_of((start // 128) * 128, 128)
    window = basis_f[:, pl.ds(base, 256)]
    pb_ref[...] = pltpu.roll(window, (256 - start % 128) % 256, 1)[:, :share]

    wg_all.wait_recv()
    w_rows = jnp.concatenate([w_full[g] for g in range(4)], axis=0)
    qt = dot_nn(inverse_terms, rows_terms(w_rows))
    qt_ref[...] = qt
    q_high = qt.astype(BF16).astype(F32)
    q3_ref[...] = jnp.concatenate([q_high, q_high, qt - q_high], axis=0).T.astype(BF16)

    for swap in swaps:
        swap.wait_send()
    plane_all.wait_send()
    z_all.wait_send()
    gather_all.wait_send()
    pair.wait_send()
    group_all.wait_send()
    wz_all.wait_send()
    wg_all.wait_send()


def error_kernel(merged_ref, basis3_ref, q3_ref, qt_ref, pb_ref, out_hbm, qt_out, pb_out, stage, sem):
    rows, width = merged_ref.shape
    cuts = [(s, min(64, rows - s)) for s in range(0, rows, 64)]
    copies = []
    for i, (s, n) in enumerate(cuts):
        block = merged_ref[s : s + n, :] - dot_nn(q3_ref[s : s + n, :], basis3_ref[...])
        stage[s : s + n, :] = block.astype(BF16)
        cp = pltpu.make_async_copy(stage.at[pl.ds(s, n)], out_hbm.at[pl.ds(s, n)], sem.at[i])
        cp.start()
        copies.append(cp)
    qt_out[...] = qt_ref[...]
    pb_out[...] = pb_ref[...]
    for cp in copies:
        cp.wait()


def body(activations, out_grads, error_memory, q_previous):
    q_t = q_previous.T
    g_t = out_grads.transpose(0, 2, 1)
    e_t = error_memory.T
    rank, columns = q_t.shape
    width = e_t.shape[0 + 1]
    tokens = activations.shape[1]
    share = width // lax.axis_size("dp")
    padded = BLOCKS * LANES
    half = rank // 2
    any_spec = pl.BlockSpec(memory_space=pl.ANY)
    vmem = pl.BlockSpec(memory_space=pltpu.VMEM)
    merged, basis3, q3, qt, pb = pl.pallas_call(
        reduce_kernel,
        out_shape=(
            jax.ShapeDtypeStruct((columns, width), F32),
            jax.ShapeDtypeStruct((3 * rank, width), BF16),
            jax.ShapeDtypeStruct((columns, 3 * rank), BF16),
            jax.ShapeDtypeStruct((rank, columns), F32),
            jax.ShapeDtypeStruct((rank, share), F32),
        ),
        in_specs=[pl.BlockSpec(memory_space=pltpu.HBM)] * 4,
        out_specs=(vmem,) * 5,
        scratch_shapes=[
            pltpu.VMEM((rank, columns), F32),
            pltpu.VMEM((columns, 2 * tokens), BF16),
            pltpu.VMEM((2 * tokens, padded), BF16),
            pltpu.VMEM((columns, padded), BF16),
            pltpu.VMEM((BLOCKS, rank, LANES), F32),
            pltpu.VMEM((BLOCKS, half, LANES), F32),
            pltpu.VMEM((BLOCKS, half, LANES), F32),
            pltpu.VMEM((BLOCKS, half, LANES), F32),
            pltpu.VMEM((8, half, LANES), F32),
            pltpu.VMEM((BLOCKS, rank, LANES), F32),
            pltpu.VMEM((columns, 3 * rank), F32),
            pltpu.VMEM((3 * rank, 2 * tokens), F32),
            pltpu.VMEM((rank, rank), F32),
            pltpu.VMEM((4, 8, columns), F32),
            pltpu.VMEM((4, 8, columns), F32),
            pltpu.VMEM((8, 8, columns), F32),
            pltpu.VMEM((4, 8, columns), F32),
            pltpu.VMEM((rank, padded), F32),
            pltpu.SemaphoreType.DMA((16,)),
            pltpu.SemaphoreType.DMA((12,)),
            pltpu.SemaphoreType.DMA((48,)),
        ],
        compiler_params=pltpu.CompilerParams(
            collective_id=0, has_side_effects=True, vmem_limit_bytes=28 << 20
        ),
        name="reduce_kernel",
    )(*[pltpu.with_memory_space_constraint(x, pltpu.HBM) for x in (q_t, g_t, activations, e_t)])
    new_t, q_out, pb_out = pl.pallas_call(
        error_kernel,
        out_shape=(
            jax.ShapeDtypeStruct((columns, width), BF16),
            jax.ShapeDtypeStruct((rank, columns), F32),
            jax.ShapeDtypeStruct((rank, share), F32),
        ),
        in_specs=[vmem] * 5,
        out_specs=(any_spec, vmem, vmem),
        scratch_shapes=[pltpu.VMEM((columns, width), BF16), pltpu.SemaphoreType.DMA((8,))],
        compiler_params=pltpu.CompilerParams(vmem_limit_bytes=20 << 20),
        name="error_kernel",
    )(merged, basis3, q3, qt, pb)
    return new_t.T, pb_out.T, q_out.T


def solution(mesh):
    in_specs = (P(None, "dp", None), P(None, "dp", "mp"), P("dp", "mp"), P("mp", None))
    out_specs = (P("dp", "mp"), P("dp", None), P("mp", None))
    return jax.shard_map(body, mesh=mesh, in_specs=in_specs, out_specs=out_specs, check_vma=False)
```

```python
import functools

import jax
import jax.numpy as jnp
from jax import lax
from jax.experimental import pallas as pl
from jax.experimental.pallas import tpu as pltpu
from jax.sharding import PartitionSpec as P

MESH = pl.DeviceIdType.MESH
F32 = jnp.float32
BF16 = jnp.bfloat16
BLOCKS = 16
LANES = 256
ROW_ORDER = (2, 3, 1, 0)
X_ORDER = (2, 3, 1, 0)
BARRIER_AT = 2
P_PARTS = 2
P_Z_ORDER = (4, 3, 5, 2, 6, 1, 7, 0)
W_Z_ORDER = (0, 1, 2, 3, 4, 5, 6, 7)


def hops(step):
    return sum(min(d, 4 - d) for d in step)


SEND_ORDER = sorted(
    ((dx, dy) for dx in range(4) for dy in range(4) if dx + dy), key=lambda step: (4, 2, 3, 1, 0)[hops(step)]
)


def split_parts(x):
    high = x.astype(BF16)
    rest = x - high.astype(F32)
    middle = rest.astype(BF16)
    return high, middle, (rest - middle.astype(F32)).astype(BF16)


def split3(x):
    return jnp.concatenate(split_parts(x), axis=0)


def factor_terms(x):
    high, middle, low = split_parts(x)
    return jnp.concatenate([high, middle, low, high, middle, high], axis=1)


def rows_terms(y):
    high, middle, low = split_parts(y)
    return jnp.concatenate([high, high, high, middle, middle, low], axis=0)


def fold3(x):
    rows = x.shape[0] // 3
    return x[:rows] + x[rows : 2 * rows] + x[2 * rows :]


def dot_nn(a, b):
    return lax.dot_general(a, b, (((1,), (0,)), ((), ())), preferred_element_type=F32)


def dot_nt(a, b, precision=None):
    return lax.dot_general(
        a, b, (((1,), (1,)), ((), ())), preferred_element_type=F32, precision=precision
    )


def inverse_factor(gram):
    n = gram.shape[0]
    rows = lax.broadcasted_iota(jnp.int32, (n, 2 * n), 0)
    columns = lax.broadcasted_iota(jnp.int32, (n, 2 * n), 1)
    identity = jnp.where(rows + n == columns, 1.0, 0.0).astype(F32)
    wide = jnp.where(columns < n, jnp.concatenate([gram, gram], axis=1), identity)
    row_index = lax.broadcasted_iota(jnp.int32, (n, 1), 0)
    for j in range(n):
        pivot = wide[j : j + 1, j : j + 1]
        scale = lax.rsqrt(pivot)
        scale = scale * (1.5 - 0.5 * pivot * scale * scale)
        row = wide[j : j + 1, :] * scale
        factor = wide[:, j : j + 1] * scale
        below = wide - factor * row
        wide = jnp.where(row_index > j, below, jnp.where(row_index == j, row, wide))
    return wide[:, n:]


def reduce_kernel(
    q_hbm, g_hbm, a_hbm, e_hbm,
    merged_ref, basis3_ref, q3_ref, qt_ref, pb_ref,
    qv, gv, av, ev,
    p_part, c_recv, x_src, x_recv, z_buf, p_full, w_acc, a_acc, inv_s,
    w_src, w_recv, w_z, w_full, basis_f,
    load_sem, ssem, rsem,
):
    rank = qv.shape[0]
    half = rank // 2
    width = e_hbm.shape[1]
    share = pb_ref.shape[1]
    dp, mp = lax.axis_index("dp"), lax.axis_index("mp")
    mz, mxh, mc = lax.div(dp, 4), lax.rem(lax.div(dp, 2), 2), lax.rem(dp, 2)
    my, mxl = lax.div(mp, 2), lax.rem(mp, 2)
    mx = mxh * 2 + mxl
    me = my * 4 + mx
    oc = 1 - mc

    xs = [lax.rem(mx + d, 4) for d in range(4)]
    ys = [lax.rem(my + d, 4) for d in range(4)]
    x_dp = [(mz * 2 + lax.div(x, 2)) * 2 + mc for x in xs]
    x_mp = [lax.rem(x, 2) for x in xs]
    plane = {(dx, dy): (x_dp[dx], ys[dy] * 2 + x_mp[dx]) for dx in range(4) for dy in range(4)}
    line = [((z * 2 + mxh) * 2 + mc, mp) for z in range(8)]
    partner = (dp + 1 - 2 * mc, mp)
    group = mxh * 2 + mc
    group_peers = {}
    for j in (1, 2, 3):
        xh, c = (1 - mxh if j >= 2 else mxh), (oc if j % 2 else mc)
        group_peers[j] = (xh * 2 + c, ((mz * 2 + xh) * 2 + c, mp))

    tokens = a_hbm.shape[1]
    padded = ev.shape[1]
    loads = [pltpu.make_async_copy(q_hbm, qv, load_sem.at[0])]
    loads[0].start()
    g_loads = []
    for m in range(2):
        cp = pltpu.make_async_copy(g_hbm.at[m], gv.at[:, pl.ds(m * tokens, tokens)], load_sem.at[1 + m])
        cp.start()
        g_loads.append(cp)
    step = padded // 4
    short = width - 3 * step
    pieces = []
    for i, dy in enumerate(ROW_ORDER):
        row = ys[dy]
        start = pl.multiple_of(row * step, step)

        def piece_copies(n, start=start, i=i):
            lanes = pl.ds(start, n)
            copies = [
                pltpu.make_async_copy(
                    a_hbm.at[m, :, lanes], av.at[pl.ds(m * tokens, tokens), lanes], load_sem.at[3 + 3 * i + m]
                )
                for m in range(2)
            ]
            copies.append(pltpu.make_async_copy(e_hbm.at[:, lanes], ev.at[:, lanes], load_sem.at[5 + 3 * i]))
            return copies

        def each(action, row=row, piece_copies=piece_copies):
            @pl.when(row < 3)
            def _():
                for cp in piece_copies(step):
                    action(cp)

            @pl.when(row == 3)
            def _():
                for cp in piece_copies(short):
                    action(cp)

        each(lambda cp: cp.start())
        pieces.append((dy, row, start, each))

    barrier = pltpu.get_barrier_semaphore()

    def greet(target):
        pl.semaphore_signal(barrier, inc=1, device_id=target, device_id_type=MESH)

    for step_xy in SEND_ORDER:
        greet(plane[step_xy])
    for z in range(8):

        @pl.when(z != mz)
        def _(z=z):
            greet(line[z])

    greet(partner)
    greet(group_peers[3][1])

    ev[:, width:] = jnp.zeros((ev.shape[0], padded - width), BF16)
    av[:, width:] = jnp.zeros((av.shape[0], padded - width), BF16)

    loads[0].wait()
    qs = split3(qv[...])
    for cp in g_loads:
        cp.wait()
    gqs = split3(fold3(dot_nn(qs, gv[...])))

    def remote(src, dst, send, recv, target):
        return pltpu.make_async_remote_copy(
            src_ref=src, dst_ref=dst, send_sem=ssem.at[send], recv_sem=rsem.at[recv],
            device_id=target, device_id_type=MESH,
        )

    def along_z(order, send):
        for z in order:

            @pl.when(z != mz)
            def _(z=z):
                send(line[z])

    mine = pl.ds(pl.multiple_of(mc * half, half), half)
    other = pl.ds(pl.multiple_of(oc * half, half), half)
    swaps = []

    cuts = [pl.ds(h * (half // P_PARTS), half // P_PARTS) for h in range(P_PARTS)]

    def to_plane(i, h):
        dy, row, _, _ = pieces[i]
        for dx in X_ORDER:
            if dx + dy > 0:
                remote(
                    x_src.at[row * 4 + xs[dx], cuts[h], :], x_recv.at[dy * 4 + dx, cuts[h], :], 1, 12 + h, plane[dx, dy]
                ).start()

    for i, (dy, row, start, each) in enumerate(pieces):
        each(lambda cp: cp.wait())
        lanes = pl.ds(start, step)
        r = fold3(dot_nn(qs, ev[:, lanes]) + dot_nn(gqs, av[:, lanes]))
        for b in range(4):
            p_part[row * 4 + b] = r[:, b * LANES : (b + 1) * LANES]
        four = pl.ds(row * 4, 4)
        swaps.append(remote(p_part.at[four, other, :], c_recv.at[four], 8 + i, 8 + i, partner))
        if i == BARRIER_AT:
            pl.semaphore_wait(barrier, 24)
            for swap in swaps[:i]:
                swap.start()
        if i >= BARRIER_AT:
            swaps[i].start()
    for i, (dy, row, start, each) in enumerate(pieces):
        four = pl.ds(row * 4, 4)
        swaps[i].wait_recv()
        x_src[four] = p_part[four, mine, :] + c_recv[four]
        to_plane(i, 0)
    for h in range(1, P_PARTS):
        for i in range(4):
            to_plane(i, h)
    plane_all = remote(x_src.at[pl.ds(1, 15)], x_recv.at[pl.ds(1, 15)], 1, 1, partner)

    for s in range(0, width, 512):
        n = min(512, width - s)
        merged_ref[:, s : s + n] = dot_nn(gv[...], av[:, s : s + n]) + ev[:, s : s + n].astype(F32)

    for h, cut in enumerate(cuts):
        arrivals = x_recv.at[pl.ds(1, 15), cut, :]
        remote(arrivals, arrivals, 1, 12 + h, partner).wait_recv()
        total = x_src[me, cut, :]
        for j in range(1, 16):
            total = total + x_recv[j, cut, :]
        z_buf[mz, cut, :] = total
        block = z_buf.at[mz, cut, :]
        along_z(P_Z_ORDER, lambda target, block=block, h=h: remote(block, block, 2, 14 + h, target).start())
    z_all = remote(z_buf.at[pl.ds(0, 7)], z_buf.at[pl.ds(0, 7)], 2, 2, partner)
    for h, cut in enumerate(cuts):
        arrivals = z_buf.at[pl.ds(0, 7), cut, :]
        remote(arrivals, arrivals, 2, 14 + h, partner).wait_recv()
        total = z_buf[0, cut, :]
        for j in range(1, 8):
            total = total + z_buf[j, cut, :]
        rows = pl.ds(pl.multiple_of(mc * half + h * (half // P_PARTS), 8), half // P_PARTS)
        p_full[me, rows, :] = total
        block = p_full.at[me, rows, :]
        for dx, dy in SEND_ORDER:
            remote(block, block, 3, 16 + dy * 4 + dx, plane[dx, dy]).start()

    def block_copy(k, recv, target):
        return remote(p_full.at[k, mine, :], p_full.at[k, mine, :], 3 if recv < 32 else 4, recv, target)

    block_copy(me, 32, partner).start()

    def use(blocks):
        w_sum, a_sum = None, None
        for k, recv in blocks:
            block_copy(k, recv, partner).wait_recv()
        for k, recv in blocks:
            rows = split3(p_full[k])
            lanes = pl.ds(pl.multiple_of(k * LANES, LANES), LANES)
            w_part = dot_nt(ev[:, lanes], rows)
            a_part = dot_nt(rows, av[:, lanes])
            w_sum = w_part if w_sum is None else w_sum + w_part
            a_sum = a_part if a_sum is None else a_sum + a_part
        return w_sum, a_sum

    waiting = [(me, 32)]
    for n, distances in enumerate(((1,), (2,), (3, 4))):
        arrived = []
        for dx, dy in SEND_ORDER:
            if hops((dx, dy)) in distances:
                k = ys[-dy % 4] * 4 + xs[-dx % 4]
                block_copy(k, 16 + dy * 4 + dx, partner).wait_recv()
                block_copy(k, 32 + dy * 4 + dx, partner).start()
                arrived.append((k, 32 + dy * 4 + dx))
        if n > 0:
            w_sum, a_sum = use(waiting)
            w_acc[...] = w_sum if n == 1 else w_acc[...] + w_sum
            a_acc[...] = a_sum if n == 1 else a_acc[...] + a_sum
            waiting = []
        waiting = waiting + arrived
    w_sum, a_sum = use(waiting)
    pas = split3(fold3(a_acc[...] + a_sum))
    wt = fold3((w_acc[...] + w_sum + dot_nt(gv[...], pas)).T)
    for g in range(4):
        w_src[g] = wt[8 * g : 8 * g + 8, :]
    gather_all = remote(x_recv.at[pl.ds(1, 15)], x_recv.at[pl.ds(1, 15)], 3, 3, partner)
    pair = remote(p_full.at[:, mine, :], p_full.at[:, mine, :], 4, 4, partner)

    columns = w_src.shape[2]
    strips = [pl.ds(0, columns)]
    for h, strip in enumerate(strips):
        for j in (2, 3, 1):
            place, target = group_peers[j]
            remote(w_src.at[place, :, strip], w_recv.at[j, :, strip], 5, 5 + 2 * h, target).start()
    group_all = remote(w_src.at[pl.ds(1, 3)], w_recv.at[pl.ds(1, 3)], 5, 5, partner)

    p_rows = jnp.concatenate([p_full[b] for b in range(BLOCKS)], axis=1)
    basis_f[...] = p_rows
    inv_s[...] = dot_nt(p_rows, p_rows, lax.Precision.HIGHEST)

    for h, strip in enumerate(strips):
        arrivals = w_recv.at[pl.ds(1, 3), :, strip]
        remote(arrivals, arrivals, 5, 5 + 2 * h, partner).wait_recv()
        w_z[mz, :, strip] = w_src[group, :, strip] + w_recv[1, :, strip] + w_recv[2, :, strip] + w_recv[3, :, strip]
        block = w_z.at[mz, :, strip]
        along_z(W_Z_ORDER, lambda target, block=block, h=h: remote(block, block, 6, h, target).start())
    wz_all = remote(w_z.at[pl.ds(0, 7)], w_z.at[pl.ds(0, 7)], 6, 6, partner)

    inv_s[...] = inverse_factor(inv_s[...])

    for h, strip in enumerate(strips):
        arrivals = w_z.at[pl.ds(0, 7), :, strip]
        remote(arrivals, arrivals, 6, h, partner).wait_recv()
        total = w_z[0, :, strip]
        for j in range(1, 8):
            total = total + w_z[j, :, strip]
        w_full[group, :, strip] = total
        block = w_full.at[group, :, strip]
        for j in (2, 3, 1):
            remote(block, block, 7, 6, group_peers[j][1]).start()
    wg_all = remote(w_recv.at[pl.ds(1, 3)], w_recv.at[pl.ds(1, 3)], 7, 6, partner)

    inverse = inv_s[...]
    inverse_terms = factor_terms(inverse * (1.0 / 32))
    basis = jnp.dot(inverse, basis_f[...], precision=lax.Precision.HIGHEST, preferred_element_type=F32)
    basis_f[...] = basis
    high = basis[:, :width].astype(BF16)
    low = (basis[:, :width] - high.astype(F32)).astype(BF16)
    basis3_ref[...] = jnp.concatenate([high, low, high], axis=0)
    start = dp * share
    base = pl.multiple_of(lax.div(start, 128) * 128, 128)
    window = basis_f[:, pl.ds(base, 256)]
    pb_ref[...] = pltpu.roll(window, lax.rem(256 - lax.rem(start, 128), 256), 1)[:, :share]

    wg_all.wait_recv()
    w_rows = jnp.concatenate([w_full[g] for g in range(4)], axis=0)
    qt = dot_nn(inverse_terms, rows_terms(w_rows))
    qt_ref[...] = qt
    q_high = qt.astype(BF16).astype(F32)
    q3_ref[...] = jnp.concatenate([q_high, q_high, qt - q_high], axis=0).T.astype(BF16)

    for swap in swaps:
        swap.wait_send()
    plane_all.wait_send()
    z_all.wait_send()
    gather_all.wait_send()
    pair.wait_send()
    group_all.wait_send()
    wz_all.wait_send()
    wg_all.wait_send()


def error_kernel(merged_ref, basis3_ref, q3_ref, qt_ref, pb_ref, out_hbm, qt_out, pb_out, stage, sem):
    rows, width = merged_ref.shape
    cuts = [(s, min(64, rows - s)) for s in range(0, rows, 64)]
    copies = []
    for i, (s, n) in enumerate(cuts):
        block = merged_ref[s : s + n, :] - dot_nn(q3_ref[s : s + n, :], basis3_ref[...])
        stage[s : s + n, :] = block.astype(BF16)
        cp = pltpu.make_async_copy(stage.at[pl.ds(s, n)], out_hbm.at[pl.ds(s, n)], sem.at[i])
        cp.start()
        copies.append(cp)
    qt_out[...] = qt_ref[...]
    pb_out[...] = pb_ref[...]
    for cp in copies:
        cp.wait()


def body(activations, out_grads, error_memory, q_previous):
    q_t = q_previous.T
    g_t = out_grads.transpose(0, 2, 1)
    e_t = error_memory.T
    rank, columns = q_t.shape
    width = e_t.shape[0 + 1]
    tokens = activations.shape[1]
    share = width // lax.axis_size("dp")
    padded = BLOCKS * LANES
    half = rank // 2
    any_spec = pl.BlockSpec(memory_space=pl.ANY)
    vmem = pl.BlockSpec(memory_space=pltpu.VMEM)
    merged, basis3, q3, qt, pb = pl.pallas_call(
        reduce_kernel,
        out_shape=(
            jax.ShapeDtypeStruct((columns, width), F32),
            jax.ShapeDtypeStruct((3 * rank, width), BF16),
            jax.ShapeDtypeStruct((columns, 3 * rank), BF16),
            jax.ShapeDtypeStruct((rank, columns), F32),
            jax.ShapeDtypeStruct((rank, share), F32),
        ),
        in_specs=[pl.BlockSpec(memory_space=pltpu.HBM)] * 4,
        out_specs=(vmem,) * 5,
        scratch_shapes=[
            pltpu.VMEM((rank, columns), F32),
            pltpu.VMEM((columns, 2 * tokens), BF16),
            pltpu.VMEM((2 * tokens, padded), BF16),
            pltpu.VMEM((columns, padded), BF16),
            pltpu.VMEM((BLOCKS, rank, LANES), F32),
            pltpu.VMEM((BLOCKS, half, LANES), F32),
            pltpu.VMEM((BLOCKS, half, LANES), F32),
            pltpu.VMEM((BLOCKS, half, LANES), F32),
            pltpu.VMEM((8, half, LANES), F32),
            pltpu.VMEM((BLOCKS, rank, LANES), F32),
            pltpu.VMEM((columns, 3 * rank), F32),
            pltpu.VMEM((3 * rank, 2 * tokens), F32),
            pltpu.VMEM((rank, rank), F32),
            pltpu.VMEM((4, 8, columns), F32),
            pltpu.VMEM((4, 8, columns), F32),
            pltpu.VMEM((8, 8, columns), F32),
            pltpu.VMEM((4, 8, columns), F32),
            pltpu.VMEM((rank, padded), F32),
            pltpu.SemaphoreType.DMA((16,)),
            pltpu.SemaphoreType.DMA((12,)),
            pltpu.SemaphoreType.DMA((48,)),
        ],
        compiler_params=pltpu.CompilerParams(
            collective_id=0, has_side_effects=True, vmem_limit_bytes=28 << 20
        ),
        name="reduce_kernel",
    )(*[pltpu.with_memory_space_constraint(x, pltpu.HBM) for x in (q_t, g_t, activations, e_t)])
    new_t, q_out, pb_out = pl.pallas_call(
        error_kernel,
        out_shape=(
            jax.ShapeDtypeStruct((columns, width), BF16),
            jax.ShapeDtypeStruct((rank, columns), F32),
            jax.ShapeDtypeStruct((rank, share), F32),
        ),
        in_specs=[vmem] * 5,
        out_specs=(any_spec, vmem, vmem),
        scratch_shapes=[pltpu.VMEM((columns, width), BF16), pltpu.SemaphoreType.DMA((8,))],
        compiler_params=pltpu.CompilerParams(vmem_limit_bytes=20 << 20),
        name="error_kernel",
    )(merged, basis3, q3, qt, pb)
    return new_t.T, pb_out.T, q_out.T


def solution(mesh):
    in_specs = (P(None, "dp", None), P(None, "dp", "mp"), P("dp", "mp"), P("mp", None))
    out_specs = (P("dp", "mp"), P("dp", None), P("mp", None))
    return jax.shard_map(body, mesh=mesh, in_specs=in_specs, out_specs=out_specs, check_vma=False)
```
